256 devices in a mesh: prow: 16 (over y_hi, z), pcol: 16 (over x, y_lo, core).
Axes of the slice: x: 4, y: 4 (y_hi: 2, y_lo: 2; y = y_hi * 2 + y_lo), z: 8, core: 2. Of those that a mesh axis runs over, the one named last changes fastest.
Arguments:
- ainv: float32 [20480, 20480], P('prow', 'pcol'), may hold values from -0.15625 to 0.15625
- panels: float32 [3, 20480, 512], P(None, ('prow', 'pcol')), may hold values from -0.8 to 0.8
- ancestors: int32 [3, 2560], P(None, ('prow', 'pcol')), may hold values from 0 to 1, as said below
- dinv: float32 [3, 512, 512], P(None, 'prow', 'pcol'), may hold values from -6 to 6
Outputs:
- u_panel: float32 [3, 20480, 512], P(None, ('prow', 'pcol'))
- diag: float32 [3, 512, 512], P(None, 'prow', 'pcol')
The draws below stay inside these ranges and needn't reach their ends.
Inputs may be any that keep to these rules, and one draw needn't show every extreme that they name: `ancestors`: each entry is 0 or 1; the share of ancestor blocks varies strongly between regions of the rows.
All inputs are finite; a program needn't handle non-finite values.
Results may differ from the reference program's by a relative error of at most 0.00007.
Values sent between devices are 32-bit elements; how exact they have to be, the bound alone decides.
A program may use at most 128 MiB of HBM per device.

```python
import jax
import jax.numpy as jnp
from jax import lax

M = 20480
S = 512
NSUP = 3
BLK = 8
N_PROW = 16
N_PCOL = 16


def draw_ancestors(key, part):
    blocks = M // BLK
    regions = (blocks + 79) // 80
    first_key, second_key = jax.random.split(jax.random.fold_in(key, 17))
    levels = jax.random.randint(first_key, (NSUP, regions), 0, 101)
    rolls = jax.random.randint(second_key, (NSUP, blocks), 0, 100)
    region_of = jnp.arange(blocks, dtype=jnp.int32) // 80
    limits = jnp.take(levels, region_of, axis=1)
    return (rolls < limits).astype(jnp.int32)


def level_of(own_key, shape, pieces, least, largest):
    gain = 1.0
    for position, blocks in pieces:
        heights = jax.random.uniform(jax.random.fold_in(jax.random.fold_in(own_key, 6), position), (blocks,), jnp.float32, least / len(pieces), largest / len(pieces))
        gain = gain * jnp.repeat(jnp.exp(heights), shape[position] // blocks).reshape((-1,) + (1,) * (len(shape) - 1 - position))
    return gain


def centred(rng, dims, scale, reach, pieces=(), kind=jnp.bfloat16):
    drawn = scale * jax.random.normal(rng, dims, jnp.float32)
    if pieces:
        drawn = drawn * level_of(rng, dims, pieces, -0.22, 0.18)
    return jnp.clip(drawn, -reach, reach).astype(kind)


def setup_inputs(seed: int = 0) -> dict:
    seeds = jax.random.split(jax.random.key(seed), 5)
    ainv = centred(seeds[0], (M, M), (M // 16) ** -0.5, 0.15625, ((0, 16), (1, 16)), jnp.float32)
    panels = centred(seeds[1], (NSUP, M, S), 0.1, 0.8, ((1, 256),), jnp.float32)
    ancestors = draw_ancestors(jax.random.fold_in(seeds[4], 71), 0)
    dinv = centred(seeds[3], (NSUP, S, S), 1.0, 6.0, ((1, 16), (2, 16)), jnp.float32)
    return dict(ainv=ainv, panels=panels, ancestors=ancestors, dinv=dinv)


def reference(ainv, panels, ancestors, dinv):
    dev_rows = M // (N_PROW * N_PCOL)
    col_width = M // N_PCOL
    stored = jnp.arange(M, dtype=jnp.int32)
    col_owner = stored // col_width
    within = stored % col_width
    row_owner = within // dev_rows
    offset = within % dev_rows
    source = ((row_owner * N_PCOL + col_owner) * dev_rows + offset).astype(jnp.int32)
    row_flags = jnp.repeat(ancestors, BLK, axis=1).astype(jnp.float32)
    masked = panels * row_flags[:, :, None]
    reordered = jnp.take(masked, source, axis=1)

    def product_of(piece):
        return jnp.dot(ainv, piece, precision=lax.Precision.HIGHEST)

    products = lax.map(product_of, reordered)
    u_panel = -(row_flags[:, :, None] * products)
    diag = dinv - jnp.einsum("srn,srm->snm", masked, u_panel, precision=lax.Precision.HIGHEST)
    return u_panel, diag
```

```python
import functools

import jax
import jax.numpy as jnp
from jax import lax
from jax.experimental import pallas as pl
from jax.experimental.pallas import tpu as pltpu
from jax.sharding import Mesh
from jax.sharding import PartitionSpec as P

F32, BF16 = jnp.float32, jnp.bfloat16
NSUP, S, BLK = 3, 512, 8
NZ, NX = 8, 4
ROWS = 80
HALF = 256
UNITS = 2 * NSUP
PIECE = S // 16
PROW = ("y_hi", "z")
PCOL = ("x", "y_lo", "core")


def remote(src, dst, send, recv, sems, device):
    return pltpu.make_async_remote_copy(
        src_ref=src,
        dst_ref=dst,
        send_sem=send.at[sems],
        recv_sem=recv.at[sems],
        device_id=device,
        device_id_type=pl.DeviceIdType.MESH,
    )


def split_bf16(value):
    high = value.astype(BF16)
    return high, (value - high.astype(F32)).astype(BF16)


def kernel(
    anc, a_hbm, panels, dinv, u_out, diag_out,
    a_f32, a_hl, gath, b_hi, b_lo, part, csum, xone, xtwo, ybuf,
    dpart, dsum, dxone, dxtwo, dybuf, dtot, wsend, wrecv,
    a_sem, ys, yr, zs, zr, cs, cr, x1s, x1r, x2s, x2r, es, er,
    dcs, dcr, dx1s, dx1r, dx2s, dx2r, des, der, ws, wr,
):
    yh, z = lax.axis_index("y_hi"), lax.axis_index("z")
    x, yl, core = lax.axis_index("x"), lax.axis_index("y_lo"), lax.axis_index("core")
    own = yh * NZ + z
    z_up, z_dn = lax.rem(z + 1, NZ), lax.rem(z + NZ - 1, NZ)
    x_up, x_dn, x_far = lax.rem(x + 1, NX), lax.rem(x + 3, NX), lax.rem(x + 2, NX)
    to_z = ({"z": z_up}, {"z": z_dn})
    to_x = ({"x": x_up}, {"x": x_dn})
    to_y, to_e, to_core = {"y_hi": 1 - yh}, {"y_lo": 1 - yl}, {"core": 1 - core}

    a_copies = [
        pltpu.make_async_copy(
            a_hbm.at[pl.ds(320 * j, 320)], a_f32.at[pl.ds(320 * j, 320)], a_sem.at[j]
        )
        for j in range(NX)
    ]
    for copy in a_copies:
        copy.start()

    barrier = pltpu.get_barrier_semaphore()
    for device in (*to_z, *to_x, to_y, to_e, to_core):
        pl.semaphore_signal(barrier, inc=1, device_id=device, device_id_type=pl.DeviceIdType.MESH)
    for u in range(UNITS):
        s, h = divmod(u, 2)
        for b in range(ROWS // BLK):
            flag = anc[s, b].astype(F32)
            rows = pl.ds(b * BLK, BLK)
            gath[u, own, rows, :] = panels[s, rows, pl.ds(h * HALF, HALF)] * flag
    pl.semaphore_wait(barrier, 7)

    def ycopy(u, block):
        return remote(gath.at[u, block], gath.at[u, block], ys, yr, (u,), to_y)

    def zcopy(u, d, q, t, back):
        gone = t + 1 if back else t
        origin = lax.rem(z + (NZ - gone if d == 0 else gone), NZ)
        side = yh if q == 0 else 1 - yh
        block = gath.at[u, side * NZ + origin]
        return remote(block, block, zs, zr, (u, d, q, t), to_z[d])

    def arrived(u, q, t):
        dirs = (0, 1) if t < 3 else (q,)
        for d in dirs:
            zcopy(u, d, q, t, True).wait_recv()

    def send_on(u, q, t):
        dirs = (0, 1) if t < 3 else (q,)
        for d in dirs:
            zcopy(u, d, q, t, False).start()

    def first_own(u):
        send_on(u, 0, 0)

    def first_other(u):
        ycopy(u, (1 - yh) * NZ + z).wait_recv()
        send_on(u, 1, 0)

    ycopy(0, own).start()
    first_own(0)
    for u in range(1, UNITS):
        ycopy(u, own).start()
    first_other(0)

    def core_part(u, j):
        return remote(part.at[u, j, :, 1 - core], csum.at[u, j], cs, cr, (u, j), to_core)

    def product(u, j):
        both = jnp.dot(a_hl[j], b_hi[...], preferred_element_type=F32)
        low = jnp.dot(a_hl[j, pl.ds(0, 320)], b_lo[...], preferred_element_type=F32)
        total = both[:320] + (both[320:] + low)
        part[u, j] = total.reshape(2, 2, ROWS, HALF)
        core_part(u, j).start()

    def x_one(v, d, c, one, sems):
        return remote(c.at[v, x_far, d], one.at[v, d], *sems, (v, d), to_x[d])

    def x_two(v, d, c, two, sems):
        return remote(c.at[v, (x_up, x_dn)[d]], two.at[v, d], *sems, (v, d), to_x[d])

    def y_last(v, c, y, sems):
        return remote(c.at[v, x, 1 - yl], y.at[v], *sems, (v,), to_e)

    def sum_stage(j, v, p, c, one, two, y, s1, s2, s3):
        if j == 0:
            for k in range(NX):
                c[v, k] = c[v, k] + p[v, k, :, core]
            for d in range(2):
                x_one(v, d, c, one, s1).start()
        elif j == 1:
            for d in range(2):
                x_one(v, d, c, one, s1).wait_recv()
                to = (x_up, x_dn)[d]
                c[v, to, d] = c[v, to, d] + one[v, d]
                x_two(v, d, c, two, s2).start()
        elif j == 2:
            for d in range(2):
                x_two(v, d, c, two, s2).wait_recv()
            c[v, x] = c[v, x] + two[v, 0] + two[v, 1]
            y_last(v, c, y, s3).start()
        else:
            y_last(v, c, y, s3).wait_recv()
            return c[v, x, yl] + y[v]

    u_args = (part, csum, xone, xtwo, ybuf, (x1s, x1r), (x2s, x2r), (es, er))
    d_args = (dpart, dsum, dxone, dxtwo, dybuf, (dx1s, dx1r), (dx2s, dx2r), (des, der))

    def core_diag(s):
        return remote(dpart.at[s, :, :, 1 - core], dsum.at[s], dcs, dcr, (s,), to_core)

    def local_diag(s):
        mine = jnp.concatenate([gath[2 * s, own], gath[2 * s + 1, own]], axis=1)
        m_hi, m_lo = split_bf16(mine)
        u_t = u_out[s].T
        u_hi, u_lo = split_bf16(u_t)
        terms = jnp.dot(u_lo, m_hi, preferred_element_type=F32)
        terms = terms + jnp.dot(u_hi, m_lo, preferred_element_type=F32)
        terms = terms + jnp.dot(u_hi, m_hi, preferred_element_type=F32)
        dpart[s] = terms.reshape(NX, 2, 2, PIECE, S)
        core_diag(s).start()

    def tick(i, carry):
        for j in range(4):

            @pl.when(i < UNITS)
            def _():
                for q in range(2):
                    if j < 3:
                        arrived(i, q, j)
                        send_on(i, q, j + 1)
                    else:
                        arrived(i, q, 3)

            @pl.when(i + 1 < UNITS)
            def _():
                if j == 0:
                    first_own(i + 1)
                elif j == 1:
                    first_other(i + 1)

            @pl.when(i == 0)
            def _():
                a_copies[j].wait()
                high, low = split_bf16(a_f32[pl.ds(320 * j, 320)])
                a_hl[j, pl.ds(0, 320)] = high
                a_hl[j, pl.ds(320, 320)] = low

            @pl.when((i >= 1) & (i <= UNITS))
            def _():
                if j == 0:
                    for k in range(4):
                        high, low = split_bf16(gath[i - 1, pl.ds(4 * k, 4)].reshape(320, HALF))
                        b_hi[pl.ds(320 * k, 320)] = high
                        b_lo[pl.ds(320 * k, 320)] = low
                product(i - 1, j)

            @pl.when((i >= 2) & (i <= UNITS + 1))
            def _():
                v = i - 2
                if j == 0:
                    for k in range(NX):
                        core_part(v, k).wait_recv()
                final = sum_stage(j, v, *u_args)
                if j == 3:
                    s, h = v // 2, lax.rem(v, 2)
                    columns = pl.ds(pl.multiple_of(h * HALF, HALF), HALF)
                    for b in range(ROWS // BLK):
                        flag = anc[s, b].astype(F32)
                        rows = pl.ds(b * BLK, BLK)
                        u_out[s, rows, columns] = -(final[b * BLK : (b + 1) * BLK] * flag)

            @pl.when((i >= 4) & (lax.rem(i, 2) == 0))
            def _():
                s = i // 2 - 2
                if j == 0:
                    core_diag(s).wait_recv()
                final = sum_stage(j, s, *d_args)
                if j == 3:
                    dtot[s] = final

        @pl.when((i >= 3) & (lax.rem(i, 2) == 1))
        def _():
            local_diag((i - 3) // 2)

        return carry

    lax.fori_loop(0, UNITS + 3, tick, 0)

    group = lax.broadcasted_iota(jnp.int32, (PIECE, 128), 1) // PIECE
    for a in range(4):
        tiles = [dtot[s, :, pl.ds(128 * a, 128)] for s in range(NSUP)]
        for b in range(4):
            block = jnp.zeros((PIECE, 128), F32)
            for s in range(NSUP):
                moved = tiles[s] if s == b else pltpu.roll(tiles[s], (s - b) % 4 * PIECE, 1)
                block = jnp.where(group == s, moved, block)
            wsend[4 * a + b] = block

    def to_owner(d):
        peer = lax.rem(own + d, 16)
        device = {"y_hi": peer // NZ, "z": lax.rem(peer, NZ)}
        return remote(wsend.at[peer], wrecv.at[d], ws, wr, (d,), device)

    for d in range(1, 16):
        to_owner(d).start()
    total = wsend[own]
    for d in range(1, 16):
        to_owner(d).wait_recv()
        total = total + wrecv[d]
    turned = total.T
    for s in range(NSUP):
        diag_out[s] = dinv[s] - turned[s * PIECE : (s + 1) * PIECE]

    for d in range(1, 16):
        to_owner(d).wait_send()

    def drain(u, carry):
        ycopy(u, own).wait_send()
        for t in range(4):
            for q in range(2):
                for d in (0, 1) if t < 3 else (q,):
                    zcopy(u, d, q, t, False).wait_send()
        for j in range(NX):
            core_part(u, j).wait_send()
        for d in range(2):
            x_one(u, d, csum, xone, (x1s, x1r)).wait_send()
            x_two(u, d, csum, xtwo, (x2s, x2r)).wait_send()
        y_last(u, csum, ybuf, (es, er)).wait_send()

        @pl.when(u < NSUP)
        def _():
            core_diag(u).wait_send()
            for d in range(2):
                x_one(u, d, dsum, dxone, (dx1s, dx1r)).wait_send()
                x_two(u, d, dsum, dxtwo, (dx2s, dx2r)).wait_send()
            y_last(u, dsum, dybuf, (des, der)).wait_send()

        return carry

    lax.fori_loop(0, UNITS, drain, 0)


def on_device(ainv, panels, ancestors, dinv):
    dma = pltpu.SemaphoreType.DMA
    vmem = pltpu.VMEM
    whole = pl.BlockSpec(memory_space=pltpu.VMEM)
    pairs = [(UNITS,), (UNITS, 2, 2, 4), (UNITS, NX), (UNITS, 2), (UNITS, 2), (UNITS,)]
    pairs += [(NSUP,), (NSUP, 2), (NSUP, 2), (NSUP,), (16,)]
    return pl.pallas_call(
        kernel,
        out_shape=(
            jax.ShapeDtypeStruct((NSUP, ROWS, S), F32),
            jax.ShapeDtypeStruct((NSUP, PIECE, PIECE), F32),
        ),
        in_specs=[
            pl.BlockSpec(memory_space=pltpu.SMEM),
            pl.BlockSpec(memory_space=pl.ANY),
            whole,
            whole,
        ],
        out_specs=(whole, whole),
        scratch_shapes=[
            vmem((1280, 1280), F32),
            vmem((NX, 640, 1280), BF16),
            vmem((UNITS, 16, ROWS, HALF), F32),
            vmem((1280, HALF), BF16),
            vmem((1280, HALF), BF16),
            vmem((UNITS, NX, 2, 2, ROWS, HALF), F32),
            vmem((UNITS, NX, 2, ROWS, HALF), F32),
            vmem((UNITS, 2, ROWS, HALF), F32),
            vmem((UNITS, 2, 2, ROWS, HALF), F32),
            vmem((UNITS, ROWS, HALF), F32),
            vmem((NSUP, NX, 2, 2, PIECE, S), F32),
            vmem((NSUP, NX, 2, PIECE, S), F32),
            vmem((NSUP, 2, PIECE, S), F32),
            vmem((NSUP, 2, 2, PIECE, S), F32),
            vmem((NSUP, PIECE, S), F32),
            vmem((NSUP, PIECE, S), F32),
            vmem((16, PIECE, 128), F32),
            vmem((16, PIECE, 128), F32),
            dma((NX,)),
            *[dma(shape) for shape in pairs for _ in range(2)],
        ],
        compiler_params=pltpu.CompilerParams(
            collective_id=0, has_side_effects=True, vmem_limit_bytes=60 * 1024 * 1024
        ),
        name="selected_inversion",
    )(ancestors, ainv, panels, dinv)


def solution(mesh):
    split = Mesh(mesh.devices.reshape(2, NZ, NX, 2, 2), PROW + PCOL)
    everywhere = PROW + PCOL
    in_specs = (
        P(PROW, PCOL),
        P(None, everywhere, None),
        P(None, everywhere),
        P(None, PROW, PCOL),
    )
    out_specs = (P(None, everywhere, None), P(None, PROW, PCOL))
    return jax.shard_map(
        on_device, mesh=split, in_specs=in_specs, out_specs=out_specs, check_vma=False
    )
```

```python
import functools

import jax
import jax.numpy as jnp
from jax import lax
from jax.experimental import pallas as pl
from jax.experimental.pallas import tpu as pltpu
from jax.sharding import Mesh
from jax.sharding import PartitionSpec as P

F32, BF16 = jnp.float32, jnp.bfloat16
NSUP, S, BLK = 3, 512, 8
NZ, NX = 8, 4
ROWS = 80
HALF = 256
UNITS = 2 * NSUP
PIECE = S // 16
CROSS = 32
PROW = ("y_hi", "z")
PCOL = ("x", "y_lo", "core")


def remote(src, dst, send, recv, sems, device):
    return pltpu.make_async_remote_copy(
        src_ref=src,
        dst_ref=dst,
        send_sem=send.at[sems],
        recv_sem=recv.at[sems],
        device_id=device,
        device_id_type=pl.DeviceIdType.MESH,
    )


def split_bf16(value):
    high = value.astype(BF16)
    return high, (value - high.astype(F32)).astype(BF16)


def kernel(
    anc, a_hbm, panels, dinv, u_out, diag_out,
    a_f32, a_hl, gath, b_hi, b_lo, part, csum, xone, xtwo, ybuf,
    dpart, dsum, dxone, dxtwo, dybuf, wsend, wrecv, rows_all, mt_hi, mt_lo,
    a_sem, ys, yr, fs, fr, zs, zr, cs, cr, x1s, x1r, x2s, x2r, es, er,
    dcs, dcr, dx1s, dx1r, dx2s, dx2r, des, der, ws, wr, gs, gr,
):
    yh, z = lax.axis_index("y_hi"), lax.axis_index("z")
    x, yl, core = lax.axis_index("x"), lax.axis_index("y_lo"), lax.axis_index("core")
    own = yh * NZ + z
    z_up, z_dn = lax.rem(z + 1, NZ), lax.rem(z + NZ - 1, NZ)
    x_up, x_dn, x_far = lax.rem(x + 1, NX), lax.rem(x + 3, NX), lax.rem(x + 2, NX)
    to_z = ({"z": z_up}, {"z": z_dn})
    to_x = ({"x": x_up}, {"x": x_dn})
    to_y, to_e, to_core = {"y_hi": 1 - yh}, {"y_lo": 1 - yl}, {"core": 1 - core}

    a_copies = [
        pltpu.make_async_copy(
            a_hbm.at[pl.ds(320 * j, 320)], a_f32.at[pl.ds(320 * j, 320)], a_sem.at[j]
        )
        for j in range(NX)
    ]
    for copy in a_copies:
        copy.start()

    barrier = pltpu.get_barrier_semaphore()
    for device in (*to_z, *to_x, to_y, to_e, to_core):
        pl.semaphore_signal(barrier, inc=1, device_id=device, device_id_type=pl.DeviceIdType.MESH)

    def mask_panels(s):
        for b in range(ROWS // BLK):
            flag = anc[s, b].astype(F32)
            rows = pl.ds(b * BLK, BLK)
            masked = panels[s, rows, :] * flag
            for h in range(2):
                gath[2 * s + h, own, rows, :] = masked[:, h * HALF : (h + 1) * HALF]
            if s > 0:
                rows_all[s - 1, x, yl, core, rows, :] = masked

    for s in range(NSUP):
        mask_panels(s)
    pl.semaphore_wait(barrier, 7)

    def origin_of(d, gone):
        return lax.rem(z + (NZ - gone if d == 0 else gone), NZ)

    def ycopy(u, block):
        return remote(gath.at[u, block], gath.at[u, block], ys, yr, (u,), to_y)

    def zcopy(u, d, q, t, back):
        side = yh if q == 0 else 1 - yh
        low, high = (0, ROWS) if q == 0 else (CROSS, ROWS)
        if t == 3:
            middle = (low + high) // 2
            low, high = (low, middle) if d == 0 else (middle, high)
        origin = origin_of(d, t + 1 if back else t)
        block = gath.at[u, side * NZ + origin, pl.ds(low, high - low)]
        return remote(block, block, zs, zr, (u, d, q, t), to_z[d])

    def across(u, k, back):
        d, t = divmod(k, 3)
        origin = origin_of(0, 4) if k == 6 else origin_of(d, t + 1)
        side = 1 - yh if back else yh
        block = gath.at[u, side * NZ + origin, pl.ds(0, CROSS)]
        return remote(block, block, fs, fr, (u, k), to_y)

    def pass_on(u, t):
        for q in range(2):
            for d in range(2):
                zcopy(u, d, q, t, True).wait_recv()
                zcopy(u, d, q, t + 1, False).start()
                if q == 0:
                    across(u, 3 * d + t, False).start()

    def first_own(u):
        for d in range(2):
            zcopy(u, d, 0, 0, False).start()

    def first_other(u):
        ycopy(u, (1 - yh) * NZ + z).wait_recv()
        for d in range(2):
            zcopy(u, d, 1, 0, False).start()

    def last_across(u):
        zcopy(u, 0, 0, 3, True).wait_recv()
        across(u, 6, False).start()

    def gathered(u):
        zcopy(u, 1, 0, 3, True).wait_recv()
        for d in range(2):
            zcopy(u, d, 1, 3, True).wait_recv()
        for k in range(7):
            across(u, k, True).wait_recv()

    first_own(0)
    for u in range(UNITS):
        ycopy(u, own).start()
    first_own(1)
    first_other(0)

    mine = rows_all.at[:, x, yl, core]

    def rows_y():
        return remote(mine, mine, gs, gr, (0,), to_e)

    def rows_x(d, step):
        if step == 0:
            block = rows_all.at[:, x, :, core]
        else:
            block = rows_all.at[:, (x_dn, x_up)[d], d, core]
        return remote(block, block, gs, gr, (1 + 2 * step + d,), to_x[d])

    def rows_core():
        block = rows_all.at[:, :, :, core]
        return remote(block, block, gs, gr, (5,), to_core)

    rows_y().start()

    def core_part(u, j):
        return remote(part.at[u, j, :, 1 - core], csum.at[u, j], cs, cr, (u, j), to_core)

    def product(u, j):
        both = jnp.dot(a_hl[j], b_hi[...], preferred_element_type=F32)
        low = jnp.dot(a_hl[j, pl.ds(0, 320)], b_lo[...], preferred_element_type=F32)
        total = both[:320] + (both[320:] + low)
        part[u, j] = total.reshape(2, 2, ROWS, HALF)
        core_part(u, j).start()

    def x_one(v, d, c, one, sems):
        return remote(c.at[v, x_far, d], one.at[v, d], *sems, (v, d), to_x[d])

    def x_two(v, d, c, two, sems):
        return remote(c.at[v, (x_up, x_dn)[d]], two.at[v, d], *sems, (v, d), to_x[d])

    def y_last(v, c, y, sems):
        return remote(c.at[v, x, 1 - yl], y.at[v], *sems, (v,), to_e)

    def sum_stage(j, v, p, c, one, two, y, s1, s2, s3):
        if j == 0:
            c[v, x_far] = c[v, x_far] + p[v, x_far, :, core]
            for d in range(2):
                x_one(v, d, c, one, s1).start()
            for k in (x_up, x_dn, x):
                c[v, k] = c[v, k] + p[v, k, :, core]
        elif j == 1:
            for d in range(2):
                x_one(v, d, c, one, s1).wait_recv()
                to = (x_up, x_dn)[d]
                c[v, to, d] = c[v, to, d] + one[v, d]
                x_two(v, d, c, two, s2).start()
        elif j == 2:
            for d in range(2):
                x_two(v, d, c, two, s2).wait_recv()
            c[v, x, 1 - yl] = c[v, x, 1 - yl] + two[v, 0, 1 - yl] + two[v, 1, 1 - yl]
            y_last(v, c, y, s3).start()
            c[v, x, yl] = c[v, x, yl] + two[v, 0, yl] + two[v, 1, yl]
        else:
            y_last(v, c, y, s3).wait_recv()
            return c[v, x, yl] + y[v]

    u_args = (part, csum, xone, xtwo, ybuf, (x1s, x1r), (x2s, x2r), (es, er))
    d_args = (dpart, dsum, dxone, dxtwo, dybuf, (dx1s, dx1r), (dx2s, dx2r), (des, der))

    def sum_unit(j, v):
        if j == 0:
            for k in range(NX):
                core_part(v, k).wait_recv()
        final = sum_stage(j, v, *u_args)
        if j == 3:
            s, h = v // 2, v % 2
            columns = pl.ds(h * HALF, HALF) if isinstance(v, int) else pl.ds(pl.multiple_of(h * HALF, HALF), HALF)
            for b in range(ROWS // BLK):
                flag = anc[s, b].astype(F32)
                rows = pl.ds(b * BLK, BLK)
                u_out[s, rows, columns] = -(final[b * BLK : (b + 1) * BLK] * flag)

    def core_diag(s):
        return remote(dpart.at[s, :, :, 1 - core], dsum.at[s], dcs, dcr, (s,), to_core)

    def local_diag(s):
        own_rows = jnp.concatenate([gath[2 * s, own], gath[2 * s + 1, own]], axis=1)
        m_hi, m_lo = split_bf16(own_rows)
        u_hi, u_lo = split_bf16(u_out[s].T)
        terms = jnp.dot(u_lo, m_hi, preferred_element_type=F32)
        terms = terms + jnp.dot(u_hi, m_lo, preferred_element_type=F32)
        terms = terms + jnp.dot(u_hi, m_hi, preferred_element_type=F32)
        dpart[s] = terms.reshape(NX, 2, 2, PIECE, S)
        core_diag(s).start()

    def turn_rows(s):
        for k in range(10):
            piece = rows_all[s - 1].reshape(1280, S)[128 * k : 128 * (k + 1)]
            high, low = split_bf16(piece.T)
            mt_hi[s - 1, :, pl.ds(128 * k, 128)] = high
            mt_lo[s - 1, :, pl.ds(128 * k, 128)] = low

    def half_diag(s, h):
        for k in range(4):
            high, low = split_bf16(part[2 * s + h, k].reshape(320, HALF))
            b_hi[pl.ds(320 * k, 320)] = high
            b_lo[pl.ds(320 * k, 320)] = low
        terms = jnp.dot(mt_lo[s - 1], b_hi[...], preferred_element_type=F32)
        terms = terms + jnp.dot(mt_hi[s - 1], b_lo[...], preferred_element_type=F32)
        terms = terms + jnp.dot(mt_hi[s - 1], b_hi[...], preferred_element_type=F32)
        dpart[s, pl.ds(2 * h, 2)] = (-terms.T).reshape(2, 2, 2, PIECE, S)

    group = lax.broadcasted_iota(jnp.int32, (BLK, 128), 1) // PIECE

    def to_owner(s, d):
        peer = lax.rem(own + d, 16)
        device = {"y_hi": peer // NZ, "z": lax.rem(peer, NZ)}
        return remote(wsend.at[s, peer], wrecv.at[s, d], ws, wr, (s, d), device)

    def send_to_owners(s, total):
        for a in range(4):
            for b in range(4):
                block = jnp.zeros((BLK, 128), F32)
                for k in range(4):
                    tile = total[k * BLK : (k + 1) * BLK, 128 * a : 128 * (a + 1)]
                    moved = tile if k == b else pltpu.roll(tile, (k - b) % 4 * PIECE, 1)
                    block = jnp.where(group == k, moved, block)
                wsend[s, 4 * a + b] = block
        for d in range(1, 16):
            to_owner(s, d).start()

    def sum_diag(j, s):
        if j == 0:
            core_diag(s).wait_recv()
        final = sum_stage(j, s, *d_args)
        if j == 3:
            send_to_owners(s, final)

    def at(condition):
        return pl.when(condition)

    def alive(u):
        return (u >= 0) & (u < UNITS)

    def tick(k, carry):
        multiplies = alive(k - 5)

        @at(alive(k - 4))
        def _():
            last_across(k - 4)

        @at(alive(k - 3))
        def _():
            pass_on(k - 3, 2)

        @at(k < UNITS)
        def _():
            first_other(k)

        @at(alive(k - 8))
        def _():
            sum_unit(3, k - 8)

        @at(k == 10)
        def _():
            sum_diag(1, 1)
            sum_diag(1, 0)

        @at(multiplies)
        def _():
            gathered(k - 5)
            for c in range(4):
                high, low = split_bf16(gath[k - 5, pl.ds(4 * c, 4)].reshape(320, HALF))
                b_hi[pl.ds(320 * c, 320)] = high
                b_lo[pl.ds(320 * c, 320)] = low
            product(k - 5, 0)

        @at(alive(k - 2))
        def _():
            pass_on(k - 2, 1)

        @at(k + 1 < UNITS)
        def _():
            first_own(k + 1)

        @at(alive(k - 6))
        def _():
            sum_unit(0, k - 6)

        @at(multiplies)
        def _():
            product(k - 5, 1)

        @at(alive(k - 1))
        def _():
            pass_on(k - 1, 0)

        @at(k <= NX)
        def _():
            rows = pl.ds(pl.multiple_of((k - 1) * 320, 320), 320)
            pltpu.make_async_copy(a_hbm.at[rows], a_f32.at[rows], a_sem.at[k - 1]).wait()
            high, low = split_bf16(a_f32[rows])
            a_hl[k - 1, pl.ds(0, 320)] = high
            a_hl[k - 1, pl.ds(320, 320)] = low

        @at(multiplies)
        def _():
            product(k - 5, 2)

        @at(alive(k - 7))
        def _():
            sum_unit(2, k - 7)

        @at(k == 10)
        def _():
            half_diag(2, 0)
            sum_diag(2, 1)
            sum_diag(2, 0)
            for c in range(4):
                high, low = split_bf16(gath[5, pl.ds(4 * c, 4)].reshape(320, HALF))
                b_hi[pl.ds(320 * c, 320)] = high
                b_lo[pl.ds(320 * c, 320)] = low

        @at(multiplies)
        def _():
            product(k - 5, 3)

        @at(alive(k - 6))
        def _():
            sum_unit(1, k - 6)

        @at(k == 6)
        def _():
            rows_core().wait_recv()
            turn_rows(1)

        @at(k == 7)
        def _():
            turn_rows(2)

        @at(k == 8)
        def _():
            half_diag(1, 0)

        @at(k == 9)
        def _():
            half_diag(1, 1)
            core_diag(1).start()
            local_diag(0)
            sum_diag(0, 1)
            sum_diag(0, 0)

        @at(k == 1)
        def _():
            rows_y().wait_recv()
            for d in range(2):
                rows_x(d, 0).start()

        @at(k == 3)
        def _():
            for d in range(2):
                rows_x(d, 0).wait_recv()
                rows_x(d, 1).start()

        @at(k == 5)
        def _():
            for d in range(2):
                rows_x(d, 1).wait_recv()
            rows_core().start()

        return carry

    lax.fori_loop(1, UNITS + 5, tick, 0)

    half_diag(2, 1)
    core_diag(2).start()
    sum_unit(0, 5)
    sum_diag(0, 2)
    sum_unit(2, 4)
    sum_diag(3, 1)
    sum_diag(3, 0)
    sum_unit(3, 3)
    sum_diag(1, 2)
    sum_unit(1, 5)
    sum_unit(3, 4)
    sum_diag(2, 2)
    sum_unit(2, 5)
    sum_diag(3, 2)
    sum_unit(3, 5)

    for s in range(NSUP):
        total = wsend[s, own]
        for d in range(1, 16):
            to_owner(s, d).wait_recv()
            total = total + wrecv[s, d]
        pieces = [total] + [pltpu.roll(total, 128 - k * PIECE, 1) for k in range(1, 4)]
        turned = jnp.concatenate(pieces, axis=0).T
        diag_out[s] = dinv[s] - turned[:PIECE]

    def drain(u, carry):
        ycopy(u, own).wait_send()
        for k in range(7):
            across(u, k, False).wait_send()
        for t in range(4):
            for q in range(2):
                for d in range(2):
                    zcopy(u, d, q, t, False).wait_send()
        for j in range(NX):
            core_part(u, j).wait_send()
        for d in range(2):
            x_one(u, d, csum, xone, (x1s, x1r)).wait_send()
            x_two(u, d, csum, xtwo, (x2s, x2r)).wait_send()
        y_last(u, csum, ybuf, (es, er)).wait_send()

        @pl.when(u < NSUP)
        def _():
            core_diag(u).wait_send()
            for d in range(2):
                x_one(u, d, dsum, dxone, (dx1s, dx1r)).wait_send()
                x_two(u, d, dsum, dxtwo, (dx2s, dx2r)).wait_send()
            y_last(u, dsum, dybuf, (des, der)).wait_send()
            for d in range(1, 16):
                to_owner(u, d).wait_send()

        return carry

    lax.fori_loop(0, UNITS, drain, 0)
    rows_y().wait_send()
    for d in range(2):
        rows_x(d, 0).wait_send()
        rows_x(d, 1).wait_send()
    rows_core().wait_send()


def on_device(ainv, panels, ancestors, dinv):
    dma = pltpu.SemaphoreType.DMA
    vmem = pltpu.VMEM
    whole = pl.BlockSpec(memory_space=pltpu.VMEM)
    pairs = [(UNITS,), (UNITS, 7), (UNITS, 2, 2, 4), (UNITS, NX), (UNITS, 2), (UNITS, 2)]
    pairs += [(UNITS,), (NSUP,), (NSUP, 2), (NSUP, 2), (NSUP,), (NSUP, 16), (6,)]
    return pl.pallas_call(
        kernel,
        out_shape=(
            jax.ShapeDtypeStruct((NSUP, ROWS, S), F32),
            jax.ShapeDtypeStruct((NSUP, PIECE, PIECE), F32),
        ),
        in_specs=[
            pl.BlockSpec(memory_space=pltpu.SMEM),
            pl.BlockSpec(memory_space=pl.ANY),
            whole,
            whole,
        ],
        out_specs=(whole, whole),
        scratch_shapes=[
            vmem((1280, 1280), F32),
            vmem((NX, 640, 1280), BF16),
            vmem((UNITS, 16, ROWS, HALF), F32),
            vmem((1280, HALF), BF16),
            vmem((1280, HALF), BF16),
            vmem((UNITS, NX, 2, 2, ROWS, HALF), F32),
            vmem((UNITS, NX, 2, ROWS, HALF), F32),
            vmem((UNITS, 2, ROWS, HALF), F32),
            vmem((UNITS, 2, 2, ROWS, HALF), F32),
            vmem((UNITS, ROWS, HALF), F32),
            vmem((NSUP, NX, 2, 2, PIECE, S), F32),
            vmem((NSUP, NX, 2, PIECE, S), F32),
            vmem((NSUP, 2, PIECE, S), F32),
            vmem((NSUP, 2, 2, PIECE, S), F32),
            vmem((NSUP, PIECE, S), F32),
            vmem((NSUP, 16, BLK, 128), F32),
            vmem((NSUP, 16, BLK, 128), F32),
            vmem((2, NX, 2, 2, ROWS, S), F32),
            vmem((2, S, 1280), BF16),
            vmem((2, S, 1280), BF16),
            dma((NX,)),
            *[dma(shape) for shape in pairs for _ in range(2)],
        ],
        compiler_params=pltpu.CompilerParams(
            collective_id=0, has_side_effects=True, vmem_limit_bytes=60 * 1024 * 1024
        ),
        name="selected_inversion",
    )(ancestors, ainv, panels, dinv)


def solution(mesh):
    split = Mesh(mesh.devices.reshape(2, NZ, NX, 2, 2), PROW + PCOL)
    everywhere = PROW + PCOL
    in_specs = (
        P(PROW, PCOL),
        P(None, everywhere, None),
        P(None, everywhere),
        P(None, PROW, PCOL),
    )
    out_specs = (P(None, everywhere, None), P(None, PROW, PCOL))
    return jax.shard_map(
        on_device, mesh=split, in_specs=in_specs, out_specs=out_specs, check_vma=False
    )
```

```python
import functools

import jax
import jax.numpy as jnp
from jax import lax
from jax.experimental import pallas as pl
from jax.experimental.pallas import tpu as pltpu
from jax.sharding import Mesh
from jax.sharding import PartitionSpec as P

F32, BF16 = jnp.float32, jnp.bfloat16
NSUP, S, BLK = 3, 512, 8
NZ, NX = 8, 4
ROWS = 80
HALF = 256
UNITS = 2 * NSUP
PIECE = S // 16
CROSS = 32
PROW = ("y_hi", "z")
PCOL = ("x", "y_lo", "core")


def remote(src, dst, send, recv, sems, device):
    return pltpu.make_async_remote_copy(
        src_ref=src,
        dst_ref=dst,
        send_sem=send.at[sems],
        recv_sem=recv.at[sems],
        device_id=device,
        device_id_type=pl.DeviceIdType.MESH,
    )


def split_bf16(value):
    high = value.astype(BF16)
    return high, (value - high.astype(F32)).astype(BF16)


def kernel(
    anc, a_hbm, panels, dinv, u_out, diag_out,
    a_f32, a_hl, gath, b_hi, b_lo, part, csum, xone, xtwo, ybuf,
    dpart, dsum, dxone, dxtwo, dybuf, wsend, wrecv, rows_all, mt_hi, mt_lo,
    a_sem, ys, yr, fs, fr, zs, zr, cs, cr, x1s, x1r, x2s, x2r, es, er,
    dcs, dcr, dx1s, dx1r, dx2s, dx2r, des, der, ws, wr, gs, gr,
):
    yh, z = lax.axis_index("y_hi"), lax.axis_index("z")
    x, yl, core = lax.axis_index("x"), lax.axis_index("y_lo"), lax.axis_index("core")
    own = yh * NZ + z
    z_up, z_dn = lax.rem(z + 1, NZ), lax.rem(z + NZ - 1, NZ)
    x_up, x_dn, x_far = lax.rem(x + 1, NX), lax.rem(x + 3, NX), lax.rem(x + 2, NX)
    to_z = ({"z": z_up}, {"z": z_dn})
    to_x = ({"x": x_up}, {"x": x_dn})
    to_y, to_e, to_core = {"y_hi": 1 - yh}, {"y_lo": 1 - yl}, {"core": 1 - core}

    a_copies = [
        pltpu.make_async_copy(
            a_hbm.at[pl.ds(320 * j, 320)], a_f32.at[pl.ds(320 * j, 320)], a_sem.at[j]
        )
        for j in range(NX)
    ]
    for copy in a_copies:
        copy.start()

    barrier = pltpu.get_barrier_semaphore()
    for device in (*to_z, *to_x, to_y, to_e, to_core):
        pl.semaphore_signal(barrier, inc=1, device_id=device, device_id_type=pl.DeviceIdType.MESH)

    def mask_panels(s):
        for b in range(ROWS // BLK):
            flag = anc[s, b].astype(F32)
            rows = pl.ds(b * BLK, BLK)
            masked = panels[s, rows, :] * flag
            for h in range(2):
                gath[2 * s + h, own, rows, :] = masked[:, h * HALF : (h + 1) * HALF]
            if s == 2:
                rows_all[x, yl, core, rows, :] = masked

    for s in range(NSUP):
        mask_panels(s)
    pl.semaphore_wait(barrier, 7)

    def origin_of(d, gone):
        return lax.rem(z + (NZ - gone if d == 0 else gone), NZ)

    def ycopy(u, block):
        return remote(gath.at[u, block], gath.at[u, block], ys, yr, (u,), to_y)

    def zcopy(u, d, q, t, back):
        side = yh if q == 0 else 1 - yh
        low, high = (0, ROWS) if q == 0 else (CROSS, ROWS)
        if t == 3:
            middle = (low + high) // 2
            low, high = (low, middle) if d == 0 else (middle, high)
        origin = origin_of(d, t + 1 if back else t)
        block = gath.at[u, side * NZ + origin, pl.ds(low, high - low)]
        return remote(block, block, zs, zr, (u, d, q, t), to_z[d])

    def across(u, k, back):
        d, t = divmod(k, 3)
        origin = origin_of(0, 4) if k == 6 else origin_of(d, t + 1)
        side = 1 - yh if back else yh
        block = gath.at[u, side * NZ + origin, pl.ds(0, CROSS)]
        return remote(block, block, fs, fr, (u, k), to_y)

    def pass_on(u, t):
        for q in range(2):
            for d in range(2):
                zcopy(u, d, q, t, True).wait_recv()
                zcopy(u, d, q, t + 1, False).start()
                if q == 0:
                    across(u, 3 * d + t, False).start()

    def first_own(u):
        for d in range(2):
            zcopy(u, d, 0, 0, False).start()

    def first_other(u):
        ycopy(u, (1 - yh) * NZ + z).wait_recv()
        for d in range(2):
            zcopy(u, d, 1, 0, False).start()

    def last_across(u):
        zcopy(u, 0, 0, 3, True).wait_recv()
        across(u, 6, False).start()

    def gathered(u):
        zcopy(u, 1, 0, 3, True).wait_recv()
        for d in range(2):
            zcopy(u, d, 1, 3, True).wait_recv()
        for k in range(7):
            across(u, k, True).wait_recv()

    first_own(0)
    for u in range(UNITS):
        ycopy(u, own).start()
    first_own(1)
    first_other(0)

    mine = rows_all.at[x, yl, core]

    def rows_y():
        return remote(mine, mine, gs, gr, (0,), to_e)

    def rows_x(d, step):
        if step == 0:
            block = rows_all.at[x, :, core]
        else:
            block = rows_all.at[(x_dn, x_up)[d], d, core]
        return remote(block, block, gs, gr, (1 + 2 * step + d,), to_x[d])

    def rows_core():
        block = rows_all.at[:, :, core]
        return remote(block, block, gs, gr, (5,), to_core)

    rows_y().start()

    def core_part(u, j):
        two = pl.ds(2 * j, 2)
        return remote(part.at[u, two, :, 1 - core], csum.at[u, two], cs, cr, (u, j), to_core)

    def product(u, j):
        both = jnp.dot(a_hl[j], b_hi[...], preferred_element_type=F32)
        low = jnp.dot(a_hl[j, pl.ds(0, 640)], b_lo[...], preferred_element_type=F32)
        total = both[:640] + (both[640:] + low)
        part[u, pl.ds(2 * j, 2)] = total.reshape(2, 2, 2, ROWS, HALF)
        core_part(u, j).start()

    def x_one(v, d, c, one, sems):
        return remote(c.at[v, x_far, d], one.at[v, d], *sems, (v, d), to_x[d])

    def x_two(v, d, c, two, sems):
        return remote(c.at[v, (x_up, x_dn)[d]], two.at[v, d], *sems, (v, d), to_x[d])

    def y_last(v, c, y, sems):
        return remote(c.at[v, x, 1 - yl], y.at[v], *sems, (v,), to_e)

    def sum_stage(j, v, p, c, one, two, y, s1, s2, s3):
        if j == 0:
            c[v, x_far] = c[v, x_far] + p[v, x_far, :, core]
            for d in range(2):
                x_one(v, d, c, one, s1).start()
            for k in (x_up, x_dn, x):
                c[v, k] = c[v, k] + p[v, k, :, core]
        elif j == 1:
            for d in range(2):
                x_one(v, d, c, one, s1).wait_recv()
                to = (x_up, x_dn)[d]
                c[v, to, d] = c[v, to, d] + one[v, d]
                x_two(v, d, c, two, s2).start()
        elif j == 2:
            for d in range(2):
                x_two(v, d, c, two, s2).wait_recv()
            c[v, x, 1 - yl] = c[v, x, 1 - yl] + two[v, 0, 1 - yl] + two[v, 1, 1 - yl]
            y_last(v, c, y, s3).start()
            c[v, x, yl] = c[v, x, yl] + two[v, 0, yl] + two[v, 1, yl]
        else:
            y_last(v, c, y, s3).wait_recv()
            return c[v, x, yl] + y[v]

    u_args = (part, csum, xone, xtwo, ybuf, (x1s, x1r), (x2s, x2r), (es, er))
    d_args = (dpart, dsum, dxone, dxtwo, dybuf, (dx1s, dx1r), (dx2s, dx2r), (des, der))

    def sum_unit(j, v):
        if j == 0:
            for k in range(2):
                core_part(v, k).wait_recv()
        final = sum_stage(j, v, *u_args)
        if j == 3:
            s, h = v // 2, v % 2
            columns = pl.ds(h * HALF, HALF) if isinstance(v, int) else pl.ds(pl.multiple_of(h * HALF, HALF), HALF)
            for b in range(ROWS // BLK):
                flag = anc[s, b].astype(F32)
                rows = pl.ds(b * BLK, BLK)
                u_out[s, rows, columns] = -(final[b * BLK : (b + 1) * BLK] * flag)

    def core_diag(s):
        return remote(dpart.at[s, :, :, 1 - core], dsum.at[s], dcs, dcr, (s,), to_core)

    def local_diag(s):
        own_rows = jnp.concatenate([gath[2 * s, own], gath[2 * s + 1, own]], axis=1)
        m_hi, m_lo = split_bf16(own_rows)
        u_hi, u_lo = split_bf16(u_out[s].T)
        terms = jnp.dot(u_lo, m_hi, preferred_element_type=F32)
        terms = terms + jnp.dot(u_hi, m_lo, preferred_element_type=F32)
        terms = terms + jnp.dot(u_hi, m_hi, preferred_element_type=F32)
        dpart[s] = terms.reshape(NX, 2, 2, PIECE, S)
        core_diag(s).start()

    def turn_rows():
        for k in range(10):
            piece = rows_all[...].reshape(1280, S)[128 * k : 128 * (k + 1)]
            high, low = split_bf16(piece.T)
            mt_hi[:, pl.ds(128 * k, 128)] = high
            mt_lo[:, pl.ds(128 * k, 128)] = low

    def half_diag(h):
        for k in range(4):
            high, low = split_bf16(part[4 + h, k].reshape(320, HALF))
            b_hi[pl.ds(320 * k, 320)] = high
            b_lo[pl.ds(320 * k, 320)] = low
        terms = jnp.dot(mt_lo[...], b_hi[...], preferred_element_type=F32)
        terms = terms + jnp.dot(mt_hi[...], b_lo[...], preferred_element_type=F32)
        terms = terms + jnp.dot(mt_hi[...], b_hi[...], preferred_element_type=F32)
        dpart[2, pl.ds(2 * h, 2)] = (-terms.T).reshape(2, 2, 2, PIECE, S)

    group = lax.broadcasted_iota(jnp.int32, (BLK, 128), 1) // PIECE

    def to_owner(s, d):
        peer = lax.rem(own + d, 16)
        device = {"y_hi": peer // NZ, "z": lax.rem(peer, NZ)}
        return remote(wsend.at[s, peer], wrecv.at[s, d], ws, wr, (s, d), device)

    def send_to_owners(s, total):
        for a in range(4):
            for b in range(4):
                block = jnp.zeros((BLK, 128), F32)
                for k in range(4):
                    tile = total[k * BLK : (k + 1) * BLK, 128 * a : 128 * (a + 1)]
                    moved = tile if k == b else pltpu.roll(tile, (k - b) % 4 * PIECE, 1)
                    block = jnp.where(group == k, moved, block)
                wsend[s, 4 * a + b] = block
        for d in range(1, 16):
            to_owner(s, d).start()

    def sum_diag(j, s):
        if j == 0:
            core_diag(s).wait_recv()
        final = sum_stage(j, s, *d_args)
        if j == 3:
            send_to_owners(s, final)

    def at(condition):
        return pl.when(condition)

    def alive(u):
        return (u >= 0) & (u < UNITS)

    def tick(k, carry):
        multiplies = alive(k - 4)

        @at(multiplies)
        def _():
            last_across(k - 4)

        @at(alive(k - 3))
        def _():
            pass_on(k - 3, 2)

        @at(k < UNITS)
        def _():
            first_other(k)

        @at(alive(k - 6))
        def _():
            sum_unit(2, k - 6)

        @at(k == 5)
        def _():
            rows_core().wait_recv()
            turn_rows()

        @at(k == 9)
        def _():
            sum_diag(2, 0)
            half_diag(0)

        @at(alive(k - 2))
        def _():
            pass_on(k - 2, 1)

        @at(k + 1 < UNITS)
        def _():
            first_own(k + 1)

        @at(alive(k - 5))
        def _():
            sum_unit(0, k - 5)

        @at(k == 8)
        def _():
            sum_diag(0, 0)

        @at(k <= NX)
        def _():
            rows = pl.ds(pl.multiple_of((k - 1) * 320, 320), 320)
            pltpu.make_async_copy(a_hbm.at[rows], a_f32.at[rows], a_sem.at[k - 1]).wait()
            high, low = split_bf16(a_f32[rows])
            half, place = (k - 1) // 2, lax.rem(k - 1, 2) * 320
            a_hl[half, pl.ds(pl.multiple_of(place, 320), 320)] = high
            a_hl[half, pl.ds(pl.multiple_of(640 + place, 320), 320)] = low

        @at(alive(k - 6))
        def _():
            sum_unit(3, k - 6)

        @at((k == 7) | (k == 9))
        def _():
            local_diag((k - 7) // 2)

        @at(k == 9)
        def _():
            sum_diag(3, 0)

        @at(multiplies)
        def _():
            gathered(k - 4)
            for c in range(4):
                high, low = split_bf16(gath[k - 4, pl.ds(4 * c, 4)].reshape(320, HALF))
                b_hi[pl.ds(320 * c, 320)] = high
                b_lo[pl.ds(320 * c, 320)] = low
            product(k - 4, 0)

        @at(alive(k - 1))
        def _():
            pass_on(k - 1, 0)

        @at(alive(k - 5))
        def _():
            sum_unit(1, k - 5)

        @at(k == 8)
        def _():
            sum_diag(1, 0)

        @at(multiplies)
        def _():
            product(k - 4, 1)

        @at(k == 1)
        def _():
            rows_y().wait_recv()
            for d in range(2):
                rows_x(d, 0).start()

        @at(k == 2)
        def _():
            for d in range(2):
                rows_x(d, 0).wait_recv()
                rows_x(d, 1).start()

        @at(k == 3)
        def _():
            for d in range(2):
                rows_x(d, 1).wait_recv()
            rows_core().start()

        return carry

    lax.fori_loop(1, UNITS + 4, tick, 0)

    sum_diag(0, 1)
    sum_unit(0, 5)
    half_diag(1)
    core_diag(2).start()
    sum_diag(1, 1)
    sum_unit(2, 4)
    sum_diag(0, 2)
    sum_unit(1, 5)
    sum_diag(2, 1)
    sum_unit(3, 4)
    sum_diag(1, 2)
    sum_diag(3, 1)
    sum_diag(2, 2)
    sum_unit(2, 5)
    sum_diag(3, 2)
    sum_unit(3, 5)

    for s in range(NSUP):
        total = wsend[s, own]
        for d in range(1, 16):
            to_owner(s, d).wait_recv()
            total = total + wrecv[s, d]
        pieces = [total] + [pltpu.roll(total, 128 - k * PIECE, 1) for k in range(1, 4)]
        turned = jnp.concatenate(pieces, axis=0).T
        diag_out[s] = dinv[s] - turned[:PIECE]

    def drain(u, carry):
        ycopy(u, own).wait_send()
        for k in range(7):
            across(u, k, False).wait_send()
        for t in range(4):
            for q in range(2):
                for d in range(2):
                    zcopy(u, d, q, t, False).wait_send()
        for j in range(2):
            core_part(u, j).wait_send()
        for d in range(2):
            x_one(u, d, csum, xone, (x1s, x1r)).wait_send()
            x_two(u, d, csum, xtwo, (x2s, x2r)).wait_send()
        y_last(u, csum, ybuf, (es, er)).wait_send()

        @pl.when(u < NSUP)
        def _():
            core_diag(u).wait_send()
            for d in range(2):
                x_one(u, d, dsum, dxone, (dx1s, dx1r)).wait_send()
                x_two(u, d, dsum, dxtwo, (dx2s, dx2r)).wait_send()
            y_last(u, dsum, dybuf, (des, der)).wait_send()
            for d in range(1, 16):
                to_owner(u, d).wait_send()

        return carry

    lax.fori_loop(0, UNITS, drain, 0)
    rows_y().wait_send()
    for d in range(2):
        rows_x(d, 0).wait_send()
        rows_x(d, 1).wait_send()
    rows_core().wait_send()


def on_device(ainv, panels, ancestors, dinv):
    dma = pltpu.SemaphoreType.DMA
    vmem = pltpu.VMEM
    whole = pl.BlockSpec(memory_space=pltpu.VMEM)
    pairs = [(UNITS,), (UNITS, 7), (UNITS, 2, 2, 4), (UNITS, 2), (UNITS, 2), (UNITS, 2)]
    pairs += [(UNITS,), (NSUP,), (NSUP, 2), (NSUP, 2), (NSUP,), (NSUP, 16), (6,)]
    return pl.pallas_call(
        kernel,
        out_shape=(
            jax.ShapeDtypeStruct((NSUP, ROWS, S), F32),
            jax.ShapeDtypeStruct((NSUP, PIECE, PIECE), F32),
        ),
        in_specs=[
            pl.BlockSpec(memory_space=pltpu.SMEM),
            pl.BlockSpec(memory_space=pl.ANY),
            whole,
            whole,
        ],
        out_specs=(whole, whole),
        scratch_shapes=[
            vmem((1280, 1280), F32),
            vmem((2, 1280, 1280), BF16),
            vmem((UNITS, 16, ROWS, HALF), F32),
            vmem((1280, HALF), BF16),
            vmem((1280, HALF), BF16),
            vmem((UNITS, NX, 2, 2, ROWS, HALF), F32),
            vmem((UNITS, NX, 2, ROWS, HALF), F32),
            vmem((UNITS, 2, ROWS, HALF), F32),
            vmem((UNITS, 2, 2, ROWS, HALF), F32),
            vmem((UNITS, ROWS, HALF), F32),
            vmem((NSUP, NX, 2, 2, PIECE, S), F32),
            vmem((NSUP, NX, 2, PIECE, S), F32),
            vmem((NSUP, 2, PIECE, S), F32),
            vmem((NSUP, 2, 2, PIECE, S), F32),
            vmem((NSUP, PIECE, S), F32),
            vmem((NSUP, 16, BLK, 128), F32),
            vmem((NSUP, 16, BLK, 128), F32),
            vmem((NX, 2, 2, ROWS, S), F32),
            vmem((S, 1280), BF16),
            vmem((S, 1280), BF16),
            dma((NX,)),
            *[dma(shape) for shape in pairs for _ in range(2)],
        ],
        compiler_params=pltpu.CompilerParams(
            collective_id=0, has_side_effects=True, vmem_limit_bytes=60 * 1024 * 1024
        ),
        name="selected_inversion",
    )(ancestors, ainv, panels, dinv)


def solution(mesh):
    split = Mesh(mesh.devices.reshape(2, NZ, NX, 2, 2), PROW + PCOL)
    everywhere = PROW + PCOL
    in_specs = (
        P(PROW, PCOL),
        P(None, everywhere, None),
        P(None, everywhere),
        P(None, PROW, PCOL),
    )
    out_specs = (P(None, everywhere, None), P(None, PROW, PCOL))
    return jax.shard_map(
        on_device, mesh=split, in_specs=in_specs, out_specs=out_specs, check_vma=False
    )
```

```python
import functools

import jax
import jax.numpy as jnp
from jax import lax
from jax.experimental import pallas as pl
from jax.experimental.pallas import tpu as pltpu
from jax.sharding import Mesh
from jax.sharding import PartitionSpec as P

F32, BF16 = jnp.float32, jnp.bfloat16
NSUP, S, BLK = 3, 512, 8
NZ, NX = 8, 4
ROWS = 80
HALF = 256
UNITS = 2 * NSUP
PIECE = S // 16
CROSS = 48
PROW = ("y_hi", "z")
PCOL = ("x", "y_lo", "core")


def remote(src, dst, send, recv, sems, device):
    return pltpu.make_async_remote_copy(
        src_ref=src,
        dst_ref=dst,
        send_sem=send.at[sems],
        recv_sem=recv.at[sems],
        device_id=device,
        device_id_type=pl.DeviceIdType.MESH,
    )


def split_bf16(value):
    high = value.astype(BF16)
    return high, (value - high.astype(F32)).astype(BF16)


def kernel(
    anc, a_hbm, panels, dinv, u_out, diag_out,
    a_f32, a_hl, gath, b_hi, b_lo, part, csum, xone, xtwo, ybuf,
    dpart, dsum, dxone, dxtwo, dybuf, wsend, wrecv, rows_all, mt_hi, mt_lo,
    a_sem, ys, yr, fs, fr, zs, zr, cs, cr, x1s, x1r, x2s, x2r, es, er,
    dcs, dcr, dx1s, dx1r, dx2s, dx2r, des, der, ws, wr, gs, gr,
):
    yh, z = lax.axis_index("y_hi"), lax.axis_index("z")
    x, yl, core = lax.axis_index("x"), lax.axis_index("y_lo"), lax.axis_index("core")
    own = yh * NZ + z
    z_up, z_dn = lax.rem(z + 1, NZ), lax.rem(z + NZ - 1, NZ)
    x_up, x_dn, x_far = lax.rem(x + 1, NX), lax.rem(x + 3, NX), lax.rem(x + 2, NX)
    to_z = ({"z": z_up}, {"z": z_dn})
    to_x = ({"x": x_up}, {"x": x_dn})
    to_y, to_e, to_core = {"y_hi": 1 - yh}, {"y_lo": 1 - yl}, {"core": 1 - core}

    a_copies = [
        pltpu.make_async_copy(
            a_hbm.at[pl.ds(320 * j, 320)], a_f32.at[pl.ds(320 * j, 320)], a_sem.at[j]
        )
        for j in range(NX)
    ]
    for copy in a_copies:
        copy.start()

    barrier = pltpu.get_barrier_semaphore()
    for device in (*to_z, *to_x, to_y, to_e, to_core):
        pl.semaphore_signal(barrier, inc=1, device_id=device, device_id_type=pl.DeviceIdType.MESH)

    def mask_panels(s):
        for b in range(ROWS // BLK):
            flag = anc[s, b].astype(F32)
            rows = pl.ds(b * BLK, BLK)
            masked = panels[s, rows, :] * flag
            for h in range(2):
                gath[2 * s + h, own, rows, :] = masked[:, h * HALF : (h + 1) * HALF]
            if s == 2:
                rows_all[x, yl, core, rows, :] = masked

    for s in range(NSUP):
        mask_panels(s)
    pl.semaphore_wait(barrier, 7)

    def origin_of(d, gone):
        return lax.rem(z + (NZ - gone if d == 0 else gone), NZ)

    def ycopy(u, block):
        return remote(gath.at[u, block], gath.at[u, block], ys, yr, (u,), to_y)

    def zcopy(u, d, q, t, back):
        side = yh if q == 0 else 1 - yh
        low, high = (0, ROWS) if q == 0 else (CROSS, ROWS)
        if t == 3:
            middle = CROSS if q == 0 else CROSS + 8
            low, high = (low, middle) if d == 0 else (middle, high)
        origin = origin_of(d, t + 1 if back else t)
        block = gath.at[u, side * NZ + origin, pl.ds(low, high - low)]
        return remote(block, block, zs, zr, (u, d, q, t), to_z[d])

    def across(u, k, back):
        d, t = divmod(k, 3)
        origin = origin_of(0, 4) if k == 6 else origin_of(d, t + 1)
        side = 1 - yh if back else yh
        block = gath.at[u, side * NZ + origin, pl.ds(0, CROSS)]
        return remote(block, block, fs, fr, (u, k), to_y)

    def pass_on(u, t):
        for q in range(2):
            for d in range(2):
                zcopy(u, d, q, t, True).wait_recv()
                zcopy(u, d, q, t + 1, False).start()
                if q == 0:
                    across(u, 3 * d + t, False).start()

    def first_own(u):
        for d in range(2):
            zcopy(u, d, 0, 0, False).start()

    def first_other(u):
        ycopy(u, (1 - yh) * NZ + z).wait_recv()
        for d in range(2):
            zcopy(u, d, 1, 0, False).start()

    def last_across(u):
        zcopy(u, 0, 0, 3, True).wait_recv()
        across(u, 6, False).start()

    def gathered(u):
        zcopy(u, 1, 0, 3, True).wait_recv()
        for d in range(2):
            zcopy(u, d, 1, 3, True).wait_recv()
        for k in range(7):
            across(u, k, True).wait_recv()

    first_own(0)
    for u in range(3):
        ycopy(u, own).start()
    first_own(1)
    first_other(0)

    mine = rows_all.at[x, yl, core]

    def rows_y():
        return remote(mine, mine, gs, gr, (0,), to_e)

    def rows_x(d, step):
        if step == 0:
            block = rows_all.at[x, :, core]
        else:
            block = rows_all.at[(x_dn, x_up)[d], d, core]
        return remote(block, block, gs, gr, (1 + 2 * step + d,), to_x[d])

    def rows_core():
        block = rows_all.at[:, :, core]
        return remote(block, block, gs, gr, (5,), to_core)

    rows_y().start()

    def core_part(u, j):
        two = pl.ds(2 * j, 2)
        return remote(part.at[u, two, :, 1 - core], csum.at[u, two], cs, cr, (u, j), to_core)

    def product(u, j):
        both = jnp.dot(a_hl[j], b_hi[...], preferred_element_type=F32)
        low = jnp.dot(a_hl[j, pl.ds(0, 640)], b_lo[...], preferred_element_type=F32)
        total = both[:640] + (both[640:] + low)
        part[u, pl.ds(2 * j, 2)] = total.reshape(2, 2, 2, ROWS, HALF)
        core_part(u, j).start()

    def x_one(v, d, c, one, sems):
        return remote(c.at[v, x_far, d], one.at[v, d], *sems, (v, d), to_x[d])

    def x_two(v, d, c, two, sems):
        return remote(c.at[v, (x_up, x_dn)[d]], two.at[v, d], *sems, (v, d), to_x[d])

    def y_last(v, c, y, sems):
        return remote(c.at[v, x, 1 - yl], y.at[v], *sems, (v,), to_e)

    def sum_stage(j, v, p, c, one, two, y, s1, s2, s3):
        if j == 0:
            c[v, x_far] = c[v, x_far] + p[v, x_far, :, core]
            for d in range(2):
                x_one(v, d, c, one, s1).start()
            for k in (x_up, x_dn, x):
                c[v, k] = c[v, k] + p[v, k, :, core]
        elif j == 1:
            for d in range(2):
                x_one(v, d, c, one, s1).wait_recv()
                to = (x_up, x_dn)[d]
                c[v, to, d] = c[v, to, d] + one[v, d]
                x_two(v, d, c, two, s2).start()
        elif j == 2:
            for d in range(2):
                x_two(v, d, c, two, s2).wait_recv()
            c[v, x, 1 - yl] = c[v, x, 1 - yl] + two[v, 0, 1 - yl] + two[v, 1, 1 - yl]
            y_last(v, c, y, s3).start()
            c[v, x, yl] = c[v, x, yl] + two[v, 0, yl] + two[v, 1, yl]
        else:
            y_last(v, c, y, s3).wait_recv()
            return c[v, x, yl] + y[v]

    u_args = (part, csum, xone, xtwo, ybuf, (x1s, x1r), (x2s, x2r), (es, er))
    d_args = (dpart, dsum, dxone, dxtwo, dybuf, (dx1s, dx1r), (dx2s, dx2r), (des, der))

    def sum_unit(j, v):
        if j == 0:
            for k in range(2):
                core_part(v, k).wait_recv()
        final = sum_stage(j, v, *u_args)
        if j == 3:
            s, h = v // 2, v % 2
            columns = pl.ds(h * HALF, HALF) if isinstance(v, int) else pl.ds(pl.multiple_of(h * HALF, HALF), HALF)
            for b in range(ROWS // BLK):
                flag = anc[s, b].astype(F32)
                rows = pl.ds(b * BLK, BLK)
                u_out[s, rows, columns] = -(final[b * BLK : (b + 1) * BLK] * flag)

    def core_diag(s):
        return remote(dpart.at[s, :, :, 1 - core], dsum.at[s], dcs, dcr, (s,), to_core)

    def local_diag(s):
        own_rows = jnp.concatenate([gath[2 * s, own], gath[2 * s + 1, own]], axis=1)
        m_hi, m_lo = split_bf16(own_rows)
        u_hi, u_lo = split_bf16(u_out[s].T)
        terms = jnp.dot(u_lo, m_hi, preferred_element_type=F32)
        terms = terms + jnp.dot(u_hi, m_lo, preferred_element_type=F32)
        terms = terms + jnp.dot(u_hi, m_hi, preferred_element_type=F32)
        dpart[s] = terms.reshape(NX, 2, 2, PIECE, S)
        core_diag(s).start()

    def turn_rows():
        for k in range(10):
            piece = rows_all[...].reshape(1280, S)[128 * k : 128 * (k + 1)]
            high, low = split_bf16(piece.T)
            mt_hi[:, pl.ds(128 * k, 128)] = high
            mt_lo[:, pl.ds(128 * k, 128)] = low

    def half_diag(h):
        for k in range(4):
            high, low = split_bf16(part[4 + h, k].reshape(320, HALF))
            b_hi[pl.ds(320 * k, 320)] = high
            b_lo[pl.ds(320 * k, 320)] = low
        terms = jnp.dot(mt_lo[...], b_hi[...], preferred_element_type=F32)
        terms = terms + jnp.dot(mt_hi[...], b_lo[...], preferred_element_type=F32)
        terms = terms + jnp.dot(mt_hi[...], b_hi[...], preferred_element_type=F32)
        dpart[2, pl.ds(2 * h, 2)] = (-terms.T).reshape(2, 2, 2, PIECE, S)

    group = lax.broadcasted_iota(jnp.int32, (BLK, 128), 1) // PIECE

    def to_owner(s, d):
        peer = lax.rem(own + d, 16)
        device = {"y_hi": peer // NZ, "z": lax.rem(peer, NZ)}
        return remote(wsend.at[s, peer], wrecv.at[s, d], ws, wr, (s, d), device)

    def send_to_owners(s, total):
        for a in range(4):
            for b in range(4):
                block = jnp.zeros((BLK, 128), F32)
                for k in range(4):
                    tile = total[k * BLK : (k + 1) * BLK, 128 * a : 128 * (a + 1)]
                    moved = tile if k == b else pltpu.roll(tile, (k - b) % 4 * PIECE, 1)
                    block = jnp.where(group == k, moved, block)
                wsend[s, 4 * a + b] = block
        for d in range(1, 16):
            to_owner(s, d).start()

    def sum_diag(j, s):
        if j == 0:
            core_diag(s).wait_recv()
        final = sum_stage(j, s, *d_args)
        if j == 3:
            send_to_owners(s, final)

    def at(condition):
        return pl.when(condition)

    def alive(u):
        return (u >= 0) & (u < UNITS)

    def tick(k, carry):
        multiplies = alive(k - 4)

        @at(multiplies)
        def _():
            last_across(k - 4)

        @at(alive(k - 3))
        def _():
            pass_on(k - 3, 2)

        @at(k < UNITS)
        def _():
            first_other(k)

        @at(alive(k - 6))
        def _():
            sum_unit(2, k - 6)

        @at(k == 5)
        def _():
            rows_core().wait_recv()
            turn_rows()

        @at(k == 9)
        def _():
            sum_diag(2, 0)
            half_diag(0)

        @at(alive(k - 2))
        def _():
            pass_on(k - 2, 1)

        @at(k + 1 < UNITS)
        def _():
            first_own(k + 1)

        @at(k + 2 < UNITS)
        def _():
            ycopy(k + 2, own).start()

        @at(alive(k - 5))
        def _():
            sum_unit(0, k - 5)

        @at(k == 8)
        def _():
            sum_diag(0, 0)

        @at(k <= NX)
        def _():
            rows = pl.ds(pl.multiple_of((k - 1) * 320, 320), 320)
            pltpu.make_async_copy(a_hbm.at[rows], a_f32.at[rows], a_sem.at[k - 1]).wait()
            high, low = split_bf16(a_f32[rows])
            half, place = (k - 1) // 2, lax.rem(k - 1, 2) * 320
            a_hl[half, pl.ds(pl.multiple_of(place, 320), 320)] = high
            a_hl[half, pl.ds(pl.multiple_of(640 + place, 320), 320)] = low

        @at(alive(k - 6))
        def _():
            sum_unit(3, k - 6)

        @at((k == 7) | (k == 9))
        def _():
            local_diag((k - 7) // 2)

        @at(k == 9)
        def _():
            sum_diag(3, 0)

        @at(multiplies)
        def _():
            gathered(k - 4)
            for c in range(4):
                high, low = split_bf16(gath[k - 4, pl.ds(4 * c, 4)].reshape(320, HALF))
                b_hi[pl.ds(320 * c, 320)] = high
                b_lo[pl.ds(320 * c, 320)] = low
            product(k - 4, 0)

        @at(alive(k - 1))
        def _():
            pass_on(k - 1, 0)

        @at(alive(k - 5))
        def _():
            sum_unit(1, k - 5)

        @at(k == 8)
        def _():
            sum_diag(1, 0)

        @at(multiplies)
        def _():
            product(k - 4, 1)

        @at(k == 1)
        def _():
            rows_y().wait_recv()
            for d in range(2):
                rows_x(d, 0).start()

        @at(k == 2)
        def _():
            for d in range(2):
                rows_x(d, 0).wait_recv()
                rows_x(d, 1).start()

        @at(k == 3)
        def _():
            for d in range(2):
                rows_x(d, 1).wait_recv()
            rows_core().start()

        return carry

    lax.fori_loop(1, UNITS + 4, tick, 0)

    sum_diag(0, 1)
    sum_unit(0, 5)
    half_diag(1)
    core_diag(2).start()
    sum_diag(1, 1)
    sum_unit(2, 4)
    sum_diag(0, 2)
    sum_unit(1, 5)
    sum_diag(2, 1)
    sum_unit(3, 4)
    sum_diag(1, 2)
    sum_diag(3, 1)
    sum_diag(2, 2)
    sum_unit(2, 5)
    sum_diag(3, 2)
    sum_unit(3, 5)

    for s in range(NSUP):
        total = wsend[s, own]
        for d in range(1, 16):
            to_owner(s, d).wait_recv()
            total = total + wrecv[s, d]
        pieces = [total] + [pltpu.roll(total, 128 - k * PIECE, 1) for k in range(1, 4)]
        turned = jnp.concatenate(pieces, axis=0).T
        diag_out[s] = dinv[s] - turned[:PIECE]

    def drain(u, carry):
        ycopy(u, own).wait_send()
        for k in range(7):
            across(u, k, False).wait_send()
        for t in range(4):
            for q in range(2):
                for d in range(2):
                    zcopy(u, d, q, t, False).wait_send()
        for j in range(2):
            core_part(u, j).wait_send()
        for d in range(2):
            x_one(u, d, csum, xone, (x1s, x1r)).wait_send()
            x_two(u, d, csum, xtwo, (x2s, x2r)).wait_send()
        y_last(u, csum, ybuf, (es, er)).wait_send()

        @pl.when(u < NSUP)
        def _():
            core_diag(u).wait_send()
            for d in range(2):
                x_one(u, d, dsum, dxone, (dx1s, dx1r)).wait_send()
                x_two(u, d, dsum, dxtwo, (dx2s, dx2r)).wait_send()
            y_last(u, dsum, dybuf, (des, der)).wait_send()
            for d in range(1, 16):
                to_owner(u, d).wait_send()

        return carry

    lax.fori_loop(0, UNITS, drain, 0)
    rows_y().wait_send()
    for d in range(2):
        rows_x(d, 0).wait_send()
        rows_x(d, 1).wait_send()
    rows_core().wait_send()


def on_device(ainv, panels, ancestors, dinv):
    dma = pltpu.SemaphoreType.DMA
    vmem = pltpu.VMEM
    whole = pl.BlockSpec(memory_space=pltpu.VMEM)
    pairs = [(UNITS,), (UNITS, 7), (UNITS, 2, 2, 4), (UNITS, 2), (UNITS, 2), (UNITS, 2)]
    pairs += [(UNITS,), (NSUP,), (NSUP, 2), (NSUP, 2), (NSUP,), (NSUP, 16), (6,)]
    return pl.pallas_call(
        kernel,
        out_shape=(
            jax.ShapeDtypeStruct((NSUP, ROWS, S), F32),
            jax.ShapeDtypeStruct((NSUP, PIECE, PIECE), F32),
        ),
        in_specs=[
            pl.BlockSpec(memory_space=pltpu.SMEM),
            pl.BlockSpec(memory_space=pl.ANY),
            whole,
            whole,
        ],
        out_specs=(whole, whole),
        scratch_shapes=[
            vmem((1280, 1280), F32),
            vmem((2, 1280, 1280), BF16),
            vmem((UNITS, 16, ROWS, HALF), F32),
            vmem((1280, HALF), BF16),
            vmem((1280, HALF), BF16),
            vmem((UNITS, NX, 2, 2, ROWS, HALF), F32),
            vmem((UNITS, NX, 2, ROWS, HALF), F32),
            vmem((UNITS, 2, ROWS, HALF), F32),
            vmem((UNITS, 2, 2, ROWS, HALF), F32),
            vmem((UNITS, ROWS, HALF), F32),
            vmem((NSUP, NX, 2, 2, PIECE, S), F32),
            vmem((NSUP, NX, 2, PIECE, S), F32),
            vmem((NSUP, 2, PIECE, S), F32),
            vmem((NSUP, 2, 2, PIECE, S), F32),
            vmem((NSUP, PIECE, S), F32),
            vmem((NSUP, 16, BLK, 128), F32),
            vmem((NSUP, 16, BLK, 128), F32),
            vmem((NX, 2, 2, ROWS, S), F32),
            vmem((S, 1280), BF16),
            vmem((S, 1280), BF16),
            dma((NX,)),
            *[dma(shape) for shape in pairs for _ in range(2)],
        ],
        compiler_params=pltpu.CompilerParams(
            collective_id=0, has_side_effects=True, vmem_limit_bytes=60 * 1024 * 1024
        ),
        name="selected_inversion",
    )(ancestors, ainv, panels, dinv)


def solution(mesh):
    split = Mesh(mesh.devices.reshape(2, NZ, NX, 2, 2), PROW + PCOL)
    everywhere = PROW + PCOL
    in_specs = (
        P(PROW, PCOL),
        P(None, everywhere, None),
        P(None, everywhere),
        P(None, PROW, PCOL),
    )
    out_specs = (P(None, everywhere, None), P(None, PROW, PCOL))
    return jax.shard_map(
        on_device, mesh=split, in_specs=in_specs, out_specs=out_specs, check_vma=False
    )
```
